512 devices in a mesh: row: 32 (over z, core), col: 16 (over y, x).
Axes of the slice: x: 4, y: 4, z: 16, core: 2. Of those that a mesh axis runs over, the one named last changes fastest.
Arguments:
- panel: float32 [16384, 256], P('row'), may hold values from -4 to 132
- trailing: float32 [16384, 16384], P('row', 'col'), may hold values from -6 to 6, as said below
Outputs:
- band_block: float32 [256, 256], replicated
- updated: float32 [16384, 16384], P('row', 'col')
The draws below stay inside these ranges and needn't reach their ends.
Inputs may be any that keep to these rules, and one draw needn't show every extreme that they name: trailing equals its own transpose.
All inputs are finite; a program needn't handle non-finite values.
Results may differ from the reference program's by a relative error of at most 0.000086.
Values sent between devices are 32-bit elements; how exact they have to be, the bound alone decides.
No kernel may reach another device: no remote copies, remote signals or barrier semaphores. Data moves between devices by JAX's collectives and lax.ppermute only.
A program may use at most 64 MiB of HBM per device.

```python
import jax
import jax.numpy as jnp
from jax import lax

M = 16384
B = 256


def draw_panel(key, part):
    noise = jnp.clip(jax.random.normal(key, (M, B), jnp.float32), -4.0, 4.0)
    diagonal = (jnp.arange(M)[:, None] == jnp.arange(B)[None, :]).astype(jnp.float32)
    return noise + diagonal * float(B // 2)


def draw_trailing(key, part):
    base = jnp.clip(jax.random.normal(key, (M, M), jnp.float32), -4.0, 4.0)
    return (base + base.T) * 0.7071067811865476


def setup_inputs(seed: int = 0) -> dict:
    key_of = jax.random.split(jax.random.key(seed), 3)
    return {
        "panel": draw_panel(jax.random.fold_in(key_of[2], 71), 0),
        "trailing": draw_trailing(jax.random.fold_in(key_of[2], 71), 0),
    }


highest = lax.Precision.HIGHEST

def product(left, right):
    return jnp.dot(left.astype(jnp.float32), right.astype(jnp.float32), precision=highest, preferred_element_type=jnp.float32)

def reflector_inverse(top_basis):
    size = top_basis.shape[0]
    shifted = jnp.eye(size, dtype=jnp.float32) + top_basis.T
    normal_eq = product(shifted.T, shifted)
    chol_factor = jnp.linalg.cholesky(normal_eq)
    return jax.scipy.linalg.cho_solve((chol_factor, True), shifted.T)

def reference(panel, trailing):
    gram = product(panel.T, panel)
    factor = jnp.linalg.cholesky(gram)
    band_block = -factor.T
    ortho = jax.scipy.linalg.solve_triangular(factor, panel.T, lower=True).T
    top_basis = ortho[:B]
    reflect = ortho + jnp.eye(M, B, dtype=jnp.float32)
    inverse_top = reflector_inverse(top_basis)
    projected = product(product(trailing, reflect), inverse_top.T)
    coupling = product(inverse_top, product(reflect.T, projected))
    correction = projected - 0.5 * product(reflect, coupling)
    updated = trailing - product(reflect, correction.T) - product(correction, reflect.T)
    return (band_block, updated)
```

```python
import jax
import jax.numpy as jnp
from jax import lax
from jax.sharding import PartitionSpec as P

highest = lax.Precision.HIGHEST


def product(left, right):
    return jnp.dot(left, right, precision=highest, preferred_element_type=jnp.float32)


def product_nt(left, right):
    return lax.dot_general(
        left, right, (((1,), (1,)), ((), ())), precision=highest, preferred_element_type=jnp.float32
    )


def product_tn(left, right):
    return lax.dot_general(
        left, right, (((0,), (0,)), ((), ())), precision=highest, preferred_element_type=jnp.float32
    )


def pair_sum(value):
    rows = lax.axis_size("row")
    return value + lax.ppermute(value, "row", [(i, i ^ 1) for i in range(rows)])


def spread(value, axis, count, groups=None):
    copies = jnp.broadcast_to(value[None], (count, *value.shape))
    return lax.all_to_all(copies, axis, 0, 0, axis_index_groups=groups)


def chips_sum(value):
    chips = lax.axis_size("row") // 2
    groups = [[2 * z + k for z in range(chips)] for k in range(2)]
    return jnp.sum(spread(pair_sum(value), "row", chips, groups), axis=0)


def from_first(value):
    rows = lax.axis_size("row")
    value = jnp.where(lax.axis_index("row") == 0, value, jnp.zeros_like(value))
    step = rows // 2
    while step >= 1:
        pairs = [(i, i + step) for i in range(0, rows, 2 * step)]
        value = value + lax.ppermute(value, "row", pairs)
        step //= 2
    return value


def to_columns(piece):
    rows, cols = lax.axis_size("row"), lax.axis_size("col")
    pairs = []
    for z in range(rows // 2):
        for k in range(2):
            for c in range(cols):
                pairs.append(((2 * z + k) * cols + c, (2 * c + k) * cols + z))
    turned = lax.ppermute(piece, ("row", "col"), pairs)
    gathered = lax.all_gather(turned, "row", axis=0, tiled=False)
    gathered = gathered.reshape(rows // 2, 2, *piece.shape).transpose(1, 0, 2, 3)
    return gathered.reshape(rows * piece.shape[0], piece.shape[1])


def body(panel, trailing):
    row_count, width = panel.shape
    cols = lax.axis_size("col")
    row_index = lax.axis_index("row")
    col_index = lax.axis_index("col")
    piece_rows = row_count // cols
    part_rows = width // cols

    panel_piece = lax.dynamic_slice_in_dim(panel, col_index * piece_rows, piece_rows, 0)
    panel_cols = to_columns(panel_piece)
    top_panel = from_first(panel[:width])

    gram_here = product_tn(panel, panel)
    gram_part = lax.dynamic_slice_in_dim(gram_here, col_index * part_rows, part_rows, 0)
    gram = spread(chips_sum(gram_part), "col", cols).reshape(width, width)
    factor = jnp.linalg.cholesky(gram)
    band_block = -factor.T

    top_add = jnp.pad(factor.T, ((0, row_count - width), (0, 0)))
    vectors = panel + jnp.where(row_index == 0, top_add, 0.0)
    top_add = jnp.pad(factor.T, ((0, panel_cols.shape[0] - width), (0, 0)))
    vector_cols = panel_cols + jnp.where(col_index == 0, top_add, 0.0)

    partial = product(trailing, vector_cols)
    inner = product_tn(vectors, partial)
    sent = jnp.concatenate(
        [partial.reshape(cols, piece_rows, width), inner.reshape(cols, part_rows, width)], axis=1
    )
    mine = jnp.sum(lax.all_to_all(sent, "col", 0, 0), axis=0)
    image_piece = mine[:piece_rows]
    image_cols = to_columns(image_piece)
    inner_part = chips_sum(mine[piece_rows:])
    shared = spread(jnp.concatenate([image_piece, inner_part], axis=0), "col", cols)
    image = shared[:, :piece_rows].reshape(row_count, width)
    inner = shared[:, piece_rows:].reshape(width, width)

    identity = jnp.eye(width, dtype=jnp.float32)
    factor_inverse = jax.scipy.linalg.solve_triangular(factor, identity, lower=True)
    shifted = identity + product_nt(factor_inverse, top_panel)
    chol_factor = jnp.linalg.cholesky(product_tn(shifted, shifted))
    inverse_top = jax.scipy.linalg.cho_solve((chol_factor, True), shifted.T)
    middle = product(product_tn(factor_inverse, inverse_top.T), factor_inverse)
    half = 0.5 * product_tn(middle, product(inner, middle))
    correction = product(image, middle) - product(vectors, half)
    correction_cols = product(image_cols, middle) - product(vector_cols, half)
    updated = (
        trailing - product_nt(vectors, correction_cols) - product_nt(correction, vector_cols)
    )
    return (band_block, updated)


def solution(mesh):
    in_specs = (P("row", None), P("row", "col"))
    out_specs = (P(), P("row", "col"))
    return jax.shard_map(body, mesh=mesh, in_specs=in_specs, out_specs=out_specs, check_vma=False)
```

```python
import functools

import jax
import jax.numpy as jnp
from jax import lax
from jax.experimental import pallas as pl
from jax.experimental.pallas import tpu as pltpu
from jax.sharding import PartitionSpec as P

highest = lax.Precision.HIGHEST


def product(left, right):
    return jnp.dot(left, right, precision=highest, preferred_element_type=jnp.float32)


def product_nt(left, right):
    return lax.dot_general(
        left, right, (((1,), (1,)), ((), ())), precision=highest, preferred_element_type=jnp.float32
    )


def product_tn(left, right):
    return lax.dot_general(
        left, right, (((0,), (0,)), ((), ())), precision=highest, preferred_element_type=jnp.float32
    )


def swapped(value):
    return lax.ppermute(value, "row", [(i, i ^ 1) for i in range(lax.axis_size("row"))])


def both_cores(value):
    other = swapped(value)
    first = lax.axis_index("row") % 2 == 0
    return jnp.where(first, value, other), jnp.where(first, other, value)


def spread(value, axis, groups=None):
    count = lax.axis_size(axis) if groups is None else len(groups[0])
    copies = jnp.broadcast_to(value[None], (count, *value.shape))
    return lax.all_to_all(copies, axis, 0, 0, axis_index_groups=groups)


def spread_chips(value):
    chips = lax.axis_size("row") // 2
    return spread(value, "row", [[2 * z + k for z in range(chips)] for k in range(2)])


def turn(piece):
    rows, cols = lax.axis_size("row"), lax.axis_size("col")
    pairs = []
    for z in range(rows // 2):
        for k in range(2):
            for c in range(cols):
                pairs.append(((2 * z + k) * cols + c, (2 * c + k) * cols + z))
    return lax.ppermute(piece, ("row", "col"), pairs)


def factor_kernel(gram_ref, top_ref, upper_ref, middle_ref, left, right, *, block):
    width = gram_ref.shape[0]
    rows = lax.broadcasted_iota(jnp.int32, (width, width), 0)
    cols = lax.broadcasted_iota(jnp.int32, (width, width), 1)
    left[:, :width] = gram_ref[...]
    left[:, width:] = jnp.where(rows == cols, 1.0, 0.0)
    right[:, :width] = top_ref[...]
    right[:, width:] = jnp.zeros((width, width), jnp.float32)
    inside = lax.broadcasted_iota(jnp.int32, (block, 1), 0)
    wide_row = lax.broadcasted_iota(jnp.int32, (block, 2 * width), 0)
    wide_col = lax.broadcasted_iota(jnp.int32, (block, 2 * width), 1)
    all_rows = lax.broadcasted_iota(jnp.int32, (width, block), 0)
    for start in range(0, width, block):
        stop = start + block
        part = left[start:stop, :]
        for j in range(block):
            column = part[:, start + j : start + j + 1]
            pivot = column[j : j + 1]
            scale = lax.rsqrt(pivot)
            scale = scale * (1.5 - 0.5 * pivot * scale * scale)
            row = part[j : j + 1, :] * scale
            part = jnp.where(inside == j, row, part - jnp.where(inside > j, column * scale, 0.0) * row)
        part = jnp.where(wide_col >= wide_row + start, part, 0.0)
        upper_ref[start:stop, :] = part[:, :width]
        if stop < width:
            left[stop:, :] = left[stop:, :] - product_tn(part[:, stop:width], part)
        side = right[start:stop, :] + part
        for j in range(block):
            column = side[:, start + j : start + j + 1]
            row = side[j : j + 1, :] / column[j : j + 1]
            side = jnp.where(inside == j, row, side - column * row)
        others = jnp.where((all_rows < start) | (all_rows >= stop), right[:, start:stop], 0.0)
        right[...] = right[...] - product(others, side)
        right[start:stop, :] = side
    middle_ref[...] = right[:, width:]

def factor(gram, top, block=32):
    width=gram.shape[0]
    sq=jax.ShapeDtypeStruct((width,width),jnp.float32)
    return pl.pallas_call(functools.partial(factor_kernel,block=block), out_shape=(sq,sq),
        scratch_shapes=[pltpu.VMEM((width,2*width),jnp.float32)]*2)(gram, top)


def body(panel, trailing):
    row_count, width = panel.shape
    rows, cols = lax.axis_size("row"), lax.axis_size("col")
    row_index = lax.axis_index("row")
    col_index = lax.axis_index("col")
    core = row_index % 2
    piece_rows = row_count // cols
    part_rows = width // cols
    half_rows = part_rows // 2

    def cut(value, start, size):
        return lax.dynamic_slice_in_dim(value, start, size, 0)

    turned = turn(cut(panel, col_index * piece_rows, piece_rows))
    gram_here = product_tn(panel, panel)
    mine = col_index * part_rows + core * half_rows
    theirs = col_index * part_rows + (1 - core) * half_rows
    received = swapped(
        jnp.concatenate([cut(gram_here, theirs, half_rows), cut(panel, theirs, half_rows)], axis=0)
    )
    gram_half = cut(gram_here, mine, half_rows) + received[:half_rows]
    top_half = jnp.where(core == 0, cut(panel, mine, half_rows), received[half_rows:])
    halves = jnp.concatenate([gram_half, top_half], axis=0)
    halves, turned = lax.optimization_barrier((halves, turned))
    gathered = lax.all_gather(turned, "row", axis=0, tiled=False)
    stacked = spread_chips(halves)
    halves = jnp.concatenate([jnp.sum(stacked[:, :half_rows], axis=0), stacked[0, half_rows:]], axis=0)
    pair = jnp.stack(both_cores(spread(halves, "col")), axis=1)
    gram = pair[:, :, :half_rows].reshape(width, width)
    top_panel = pair[:, :, half_rows:].reshape(width, width)
    upper, middle = factor(gram, top_panel)
    band_block = -upper

    panel_cols = gathered.reshape(rows // 2, 2, piece_rows, width).transpose(1, 0, 2, 3)
    panel_cols = panel_cols.reshape(rows * piece_rows, width)
    top_add = jnp.pad(upper, ((0, row_count - width), (0, 0)))
    vectors = panel + jnp.where(row_index == 0, top_add, 0.0)
    top_add = jnp.pad(upper, ((0, panel_cols.shape[0] - width), (0, 0)))
    vector_cols = panel_cols + jnp.where(col_index == 0, top_add, 0.0)

    partial = product(trailing, vector_cols)
    inner = product_tn(vectors, partial)
    sent = jnp.concatenate(
        [partial.reshape(cols, piece_rows, width), inner.reshape(cols, part_rows, width)], axis=1
    )
    summed = jnp.sum(lax.all_to_all(sent, "col", 0, 0), axis=0)
    image_piece = summed[:piece_rows]
    inner_part = summed[piece_rows:]
    image_turned = turn(image_piece)
    inner_part = jnp.sum(spread_chips(inner_part + swapped(inner_part)), axis=0)
    shared = spread(jnp.concatenate([image_piece, inner_part], axis=0), "col")
    image = shared[:, :piece_rows].reshape(row_count, width)
    inner = shared[:, piece_rows:].reshape(width, width)
    image_cols = spread_chips(image_turned).reshape(row_count, width)
    image_cols = jnp.concatenate(both_cores(image_cols), axis=0)

    half = 0.5 * product_tn(middle, product(inner, middle))
    correction = product(image, middle) - product(vectors, half)
    correction_cols = product(image_cols, middle) - product(vector_cols, half)
    updated = (
        trailing - product_nt(vectors, correction_cols) - product_nt(correction, vector_cols)
    )
    return (band_block, updated)


def solution(mesh):
    in_specs = (P("row", None), P("row", "col"))
    out_specs = (P(), P("row", "col"))
    return jax.shard_map(body, mesh=mesh, in_specs=in_specs, out_specs=out_specs, check_vma=False)
```

```python
import functools

import jax
import jax.numpy as jnp
from jax import lax
from jax.experimental import pallas as pl
from jax.experimental.pallas import tpu as pltpu
from jax.sharding import PartitionSpec as P

highest = lax.Precision.HIGHEST


def product(left, right):
    return jnp.dot(left, right, precision=highest, preferred_element_type=jnp.float32)


def product_nt(left, right):
    return lax.dot_general(
        left, right, (((1,), (1,)), ((), ())), precision=highest, preferred_element_type=jnp.float32
    )


def product_tn(left, right):
    return lax.dot_general(
        left, right, (((0,), (0,)), ((), ())), precision=highest, preferred_element_type=jnp.float32
    )


def swapped(value):
    return lax.ppermute(value, "row", [(i, i ^ 1) for i in range(lax.axis_size("row"))])


def both_cores(value):
    other = swapped(value)
    first = lax.axis_index("row") % 2 == 0
    return jnp.where(first, value, other), jnp.where(first, other, value)


def spread(value, axis):
    copies = jnp.broadcast_to(value[None], (lax.axis_size(axis), *value.shape))
    return lax.all_to_all(copies, axis, 0, 0)


def gather_chips(value):
    chips = lax.axis_size("row") // 2
    groups = [[2 * z + k for z in range(chips)] for k in range(2)]
    return lax.all_gather(value, "row", axis=0, tiled=False, axis_index_groups=groups)


def turn(piece):
    rows, cols = lax.axis_size("row"), lax.axis_size("col")
    pairs = []
    for z in range(rows // 2):
        for k in range(2):
            for c in range(cols):
                pairs.append(((2 * z + k) * cols + c, (2 * c + k) * cols + z))
    return lax.ppermute(piece, ("row", "col"), pairs)


def factor_kernel(gram_ref, top_ref, upper_ref, middle_ref, left, right, *, block):
    width = gram_ref.shape[0]
    rows = lax.broadcasted_iota(jnp.int32, (width, width), 0)
    cols = lax.broadcasted_iota(jnp.int32, (width, width), 1)
    left[:, :width] = gram_ref[...]
    left[:, width:] = jnp.where(rows == cols, 1.0, 0.0)
    right[:, :width] = top_ref[...]
    right[:, width:] = jnp.zeros((width, width), jnp.float32)
    inside = lax.broadcasted_iota(jnp.int32, (block, 1), 0)
    wide_row = lax.broadcasted_iota(jnp.int32, (block, 2 * width), 0)
    wide_col = lax.broadcasted_iota(jnp.int32, (block, 2 * width), 1)
    all_rows = lax.broadcasted_iota(jnp.int32, (width, block), 0)
    for start in range(0, width, block):
        stop = start + block
        part = left[start:stop, :]
        for j in range(block):
            column = part[:, start + j : start + j + 1]
            pivot = column[j : j + 1]
            scale = lax.rsqrt(pivot)
            scale = scale * (1.5 - 0.5 * pivot * scale * scale)
            row = part[j : j + 1, :] * scale
            part = jnp.where(inside == j, row, part - jnp.where(inside > j, column * scale, 0.0) * row)
        part = jnp.where(wide_col >= wide_row + start, part, 0.0)
        upper_ref[start:stop, :] = part[:, :width]
        if stop < width:
            left[stop:, :] = left[stop:, :] - product_tn(part[:, stop:width], part)
        side = right[start:stop, :] + part
        for j in range(block):
            column = side[:, start + j : start + j + 1]
            row = side[j : j + 1, :] / column[j : j + 1]
            side = jnp.where(inside == j, row, side - column * row)
        others = jnp.where((all_rows < start) | (all_rows >= stop), right[:, start:stop], 0.0)
        right[...] = right[...] - product(others, side)
        right[start:stop, :] = side
    middle_ref[...] = right[:, width:]

def factor(gram, top, block=32):
    width=gram.shape[0]
    sq=jax.ShapeDtypeStruct((width,width),jnp.float32)
    return pl.pallas_call(functools.partial(factor_kernel,block=block), out_shape=(sq,sq),
        scratch_shapes=[pltpu.VMEM((width,2*width),jnp.float32)]*2)(gram, top)


def body(panel, trailing):
    row_count, width = panel.shape
    cols = lax.axis_size("col")
    row_index = lax.axis_index("row")
    col_index = lax.axis_index("col")
    core = row_index % 2
    piece_rows = row_count // cols
    part_rows = width // cols
    half_rows = part_rows // 2

    def cut(value, start, size):
        return lax.dynamic_slice_in_dim(value, start, size, 0)

    turned = turn(cut(panel, col_index * piece_rows, piece_rows))
    gram_here = product_tn(panel, panel)
    mine = col_index * part_rows + core * half_rows
    theirs = col_index * part_rows + (1 - core) * half_rows
    received = swapped(
        jnp.concatenate([cut(gram_here, theirs, half_rows), cut(panel, theirs, half_rows)], axis=0)
    )
    gram_half = cut(gram_here, mine, half_rows) + received[:half_rows]
    top_half = jnp.where(core == 0, cut(panel, mine, half_rows), received[half_rows:])
    stacked = gather_chips(jnp.concatenate([turned, gram_half, top_half], axis=0))
    panel_cols = stacked[:, :piece_rows].reshape(row_count, width)
    panel_cols = jnp.concatenate(both_cores(panel_cols), axis=0)
    gram_half = jnp.sum(stacked[:, piece_rows : piece_rows + half_rows], axis=0)
    halves = jnp.concatenate([gram_half, stacked[0, piece_rows + half_rows :]], axis=0)
    pair = jnp.stack(both_cores(spread(halves, "col")), axis=1)
    gram = pair[:, :, :half_rows].reshape(width, width)
    top_panel = pair[:, :, half_rows:].reshape(width, width)
    upper, middle = factor(gram, top_panel)
    band_block = -upper

    top_add = jnp.pad(upper, ((0, row_count - width), (0, 0)))
    vectors = panel + jnp.where(row_index == 0, top_add, 0.0)
    top_add = jnp.pad(upper, ((0, panel_cols.shape[0] - width), (0, 0)))
    vector_cols = panel_cols + jnp.where(col_index == 0, top_add, 0.0)

    partial = product(trailing, vector_cols)
    inner = product_tn(vectors, partial)
    sent = jnp.concatenate(
        [partial.reshape(cols, piece_rows, width), inner.reshape(cols, part_rows, width)], axis=1
    )
    summed = jnp.sum(lax.all_to_all(sent, "col", 0, 0), axis=0)
    image_piece = summed[:piece_rows]
    inner_part = summed[piece_rows:]
    image_turned = turn(image_piece)
    inner_part = inner_part + swapped(inner_part)
    stacked = gather_chips(jnp.concatenate([image_turned, inner_part], axis=0))
    image_cols = stacked[:, :piece_rows].reshape(row_count, width)
    image_cols = jnp.concatenate(both_cores(image_cols), axis=0)
    inner_part = jnp.sum(stacked[:, piece_rows:], axis=0)
    shared = spread(jnp.concatenate([image_piece, inner_part], axis=0), "col")
    image = shared[:, :piece_rows].reshape(row_count, width)
    inner = shared[:, piece_rows:].reshape(width, width)

    half = 0.5 * product_tn(middle, product(inner, middle))
    correction = product(image, middle) - product(vectors, half)
    correction_cols = product(image_cols, middle) - product(vector_cols, half)
    updated = (
        trailing - product_nt(vectors, correction_cols) - product_nt(correction, vector_cols)
    )
    return (band_block, updated)


def solution(mesh):
    in_specs = (P("row", None), P("row", "col"))
    out_specs = (P(), P("row", "col"))
    return jax.shard_map(body, mesh=mesh, in_specs=in_specs, out_specs=out_specs, check_vma=False)
```

```python
import functools

import jax
import jax.numpy as jnp
from jax import lax
from jax.experimental import pallas as pl
from jax.experimental.pallas import tpu as pltpu
from jax.sharding import PartitionSpec as P

highest = lax.Precision.HIGHEST
high = lax.Precision.HIGH


def product(left, right, precision=highest):
    return jnp.dot(left, right, precision=precision, preferred_element_type=jnp.float32)


def product_nt(left, right, precision=highest):
    return lax.dot_general(
        left,
        right,
        (((1,), (1,)), ((), ())),
        precision=precision,
        preferred_element_type=jnp.float32,
    )


def product_tn(left, right):
    return lax.dot_general(
        left, right, (((0,), (0,)), ((), ())), precision=highest, preferred_element_type=jnp.float32
    )


def swapped(value):
    return lax.ppermute(value, "row", [(i, i ^ 1) for i in range(lax.axis_size("row"))])


def both_cores(value):
    other = swapped(value)
    first = lax.axis_index("row") % 2 == 0
    return jnp.where(first, value, other), jnp.where(first, other, value)


def spread(value, own):
    copies = jnp.broadcast_to(value[None], (own.shape[0], *value.shape))
    return lax.all_to_all(jnp.concatenate([own, copies], axis=1), "col", 0, 0)


def gather_chips(value):
    chips = lax.axis_size("row") // 2
    groups = [[2 * z + k for z in range(chips)] for k in range(2)]
    return lax.all_gather(value, "row", axis=0, tiled=False, axis_index_groups=groups)


lanes = 128


def tiled(value, width):
    return jnp.concatenate([value] * (width // lanes), axis=1)


class Sweep:
    def __init__(self, panel, start, below, sub):
        self.panel, self.start, self.below, self.sub = panel, start, below, sub
        self.rows = panel.shape[0]
        self.place = lax.broadcasted_iota(jnp.int32, (self.rows, lanes), 0)
        self.pivots = jnp.zeros((self.rows, lanes), jnp.float32)

    def step(self, j):
        k = j % self.sub
        if k == 0:
            self.columns = [
                jnp.broadcast_to(self.panel[:, self.start + j + i : self.start + j + i + 1], (self.rows, lanes))
                for i in range(self.sub)
            ]
        column = self.columns[k]
        pivot = column[j : j + 1]
        keep = self.place > j if self.below else self.place != j
        ratio = jnp.where(keep, column * (1.0 / pivot), 0.0)
        for i in range(k + 1, self.sub):
            self.columns[i] = self.columns[i] - ratio * self.columns[i][j : j + 1]
        self.panel = self.panel - tiled(ratio, self.panel.shape[1]) * self.panel[j : j + 1]
        self.pivots = jnp.where(self.place == j, pivot, self.pivots)


def factor_kernel(gram_ref, top_ref, upper_ref, middle_ref, left, right, *, block, sub):
    width = gram_ref.shape[0]
    rows = lax.broadcasted_iota(jnp.int32, (width, width), 0)
    cols = lax.broadcasted_iota(jnp.int32, (width, width), 1)
    left[:, :width] = gram_ref[...]
    left[:, width:] = jnp.where(rows == cols, 1.0, 0.0)
    right[:, :width] = top_ref[...]
    right[:, width:] = jnp.zeros((width, width), jnp.float32)
    wide_row = lax.broadcasted_iota(jnp.int32, (block, 2 * width), 0)
    wide_col = lax.broadcasted_iota(jnp.int32, (block, 2 * width), 1)
    all_rows = lax.broadcasted_iota(jnp.int32, (width, block), 0)
    side = None
    for start in range(0, width + block, block):
        stop = start + block
        sweeps = []
        if start < width:
            sweeps.append(Sweep(left[start:stop, :], start, True, sub))
        if start:
            sweeps.append(Sweep(side, start - block, False, sub))
        for j in range(block):
            for sweep in sweeps:
                sweep.step(j)
        if start:
            old = start - block
            side = sweeps[-1].panel * tiled(1.0 / sweeps[-1].pivots, 2 * width)
            others = jnp.where((all_rows < old) | (all_rows >= start), right[:, old:start], 0.0)
            right[...] = right[...] - product(others, side)
            right[old:start, :] = side
        if start < width:
            pivots = sweeps[0].pivots
            scale = lax.rsqrt(pivots)
            scale = scale * (1.5 - 0.5 * pivots * scale * scale)
            part = jnp.where(wide_col >= wide_row + start, sweeps[0].panel * tiled(scale, 2 * width), 0.0)
            upper_ref[start:stop, :] = part[:, :width]
            if stop < width:
                left[stop:, :] = left[stop:, :] - product_tn(part[:, stop:width], part)
            side = right[start:stop, :] + part
    middle_ref[...] = right[:, width:]


def factor(gram, top):
    width = gram.shape[0]
    square = jax.ShapeDtypeStruct((width, width), jnp.float32)
    return pl.pallas_call(
        functools.partial(factor_kernel, block=64, sub=8),
        out_shape=(square, square),
        scratch_shapes=[pltpu.VMEM((width, 2 * width), jnp.float32)] * 2,
    )(gram, top)


def body(panel, trailing):
    row_count, width = panel.shape
    cols = lax.axis_size("col")
    row_index = lax.axis_index("row")
    col_index = lax.axis_index("col")
    core = row_index % 2
    piece_rows = row_count // cols
    part_rows = width // cols
    half_rows = part_rows // 2

    def cut(value, start, size):
        return lax.dynamic_slice_in_dim(value, start, size, 0)

    panel_piece = cut(panel, col_index * piece_rows, piece_rows)
    gram_here = product_tn(panel, panel)
    mine = col_index * part_rows + core * half_rows
    theirs = col_index * part_rows + (1 - core) * half_rows
    received = swapped(
        jnp.concatenate([cut(gram_here, theirs, half_rows), cut(panel, theirs, half_rows)], axis=0)
    )
    gram_half = cut(gram_here, mine, half_rows) + received[:half_rows]
    top_half = jnp.where(core == 0, cut(panel, mine, half_rows), received[half_rows:])
    stacked = gather_chips(jnp.concatenate([panel_piece, gram_half, top_half], axis=0))
    gram_half = jnp.sum(stacked[:, piece_rows : piece_rows + half_rows], axis=0)
    halves = jnp.concatenate([gram_half, stacked[0, piece_rows + half_rows :]], axis=0)
    received = spread(halves, stacked[:, :piece_rows])
    pair = jnp.stack(both_cores(received[:, piece_rows:]), axis=1)
    gram = pair[:, :, :half_rows].reshape(width, width)
    top_panel = pair[:, :, half_rows:].reshape(width, width)
    panel_cols = received[:, :piece_rows].reshape(row_count, width)
    panel_cols = jnp.concatenate(both_cores(panel_cols), axis=0)
    upper, middle = factor(gram, top_panel)
    band_block = -upper

    top_add = jnp.pad(upper, ((0, row_count - width), (0, 0)))
    vectors = panel + jnp.where(row_index == 0, top_add, 0.0)
    top_add = jnp.pad(upper, ((0, panel_cols.shape[0] - width), (0, 0)))
    vector_cols = panel_cols + jnp.where(col_index == 0, top_add, 0.0)

    partial = product(trailing, vector_cols, high)
    inner = product_tn(vectors, partial)
    sent = jnp.concatenate(
        [partial.reshape(cols, piece_rows, width), inner.reshape(cols, part_rows, width)], axis=1
    )
    summed = jnp.sum(lax.all_to_all(sent, "col", 0, 0), axis=0)
    image_piece = summed[:piece_rows]
    inner_part = summed[piece_rows:]
    inner_part = inner_part + swapped(inner_part)
    stacked = gather_chips(jnp.concatenate([image_piece, inner_part], axis=0))
    inner_part = jnp.sum(stacked[:, piece_rows:], axis=0)
    received = spread(
        jnp.concatenate([image_piece, inner_part], axis=0), stacked[:, :piece_rows]
    )
    image_cols = received[:, :piece_rows].reshape(row_count, width)
    image_cols = jnp.concatenate(both_cores(image_cols), axis=0)
    image = received[:, piece_rows : 2 * piece_rows].reshape(row_count, width)
    inner = received[:, 2 * piece_rows :].reshape(width, width)

    half = 0.5 * product_tn(middle, product(inner, middle))
    correction = product(image, middle) - product(vectors, half)
    correction_cols = product(image_cols, middle) - product(vector_cols, half)
    updated = (
        trailing
        - product_nt(vectors, correction_cols, high)
        - product_nt(correction, vector_cols, high)
    )
    return (band_block, updated)


def solution(mesh):
    in_specs = (P("row", None), P("row", "col"))
    out_specs = (P(), P("row", "col"))
    return jax.shard_map(body, mesh=mesh, in_specs=in_specs, out_specs=out_specs, check_vma=False)
```

```python
import functools

import jax
import jax.numpy as jnp
from jax import lax
from jax.experimental import pallas as pl
from jax.experimental.pallas import tpu as pltpu
from jax.sharding import PartitionSpec as P

highest = lax.Precision.HIGHEST
high = lax.Precision.HIGH


def product(left, right, precision=highest):
    return jnp.dot(left, right, precision=precision, preferred_element_type=jnp.float32)


def product_nt(left, right, precision=highest):
    return lax.dot_general(
        left,
        right,
        (((1,), (1,)), ((), ())),
        precision=precision,
        preferred_element_type=jnp.float32,
    )


def product_tn(left, right):
    return lax.dot_general(
        left, right, (((0,), (0,)), ((), ())), precision=highest, preferred_element_type=jnp.float32
    )


def swapped(value):
    return lax.ppermute(value, "row", [(i, i ^ 1) for i in range(lax.axis_size("row"))])


def both_cores(value):
    other = swapped(value)
    first = lax.axis_index("row") % 2 == 0
    return jnp.where(first, value, other), jnp.where(first, other, value)


def spread(value, own):
    copies = jnp.broadcast_to(value[None], (own.shape[0], *value.shape))
    return lax.all_to_all(jnp.concatenate([own, copies], axis=1), "col", 0, 0)


def gather_chips(value):
    chips = lax.axis_size("row") // 2
    groups = [[2 * z + k for z in range(chips)] for k in range(2)]
    return lax.all_gather(value, "row", axis=0, tiled=False, axis_index_groups=groups)


lanes = 128


def tiled(value, width):
    return jnp.concatenate([value] * (width // lanes), axis=1)


class Sweep:
    def __init__(self, panel, start, below, sub):
        self.panel, self.start, self.below, self.sub = panel, start, below, sub
        self.rows = panel.shape[0]
        self.place = lax.broadcasted_iota(jnp.int32, (self.rows, lanes), 0)
        self.pivots = jnp.zeros((self.rows, lanes), jnp.float32)

    def step(self, j):
        k = j % self.sub
        if k == 0:
            self.columns = [
                jnp.broadcast_to(self.panel[:, self.start + j + i : self.start + j + i + 1], (self.rows, lanes))
                for i in range(self.sub)
            ]
        column = self.columns[k]
        pivot = column[j : j + 1]
        keep = self.place > j if self.below else self.place != j
        ratio = jnp.where(keep, column * (1.0 / pivot), 0.0)
        for i in range(k + 1, self.sub):
            self.columns[i] = self.columns[i] - ratio * self.columns[i][j : j + 1]
        self.panel = self.panel - tiled(ratio, self.panel.shape[1]) * self.panel[j : j + 1]
        self.pivots = jnp.where(self.place == j, pivot, self.pivots)


def factor_kernel(gram_ref, top_ref, upper_ref, middle_ref, left, right, *, block, sub):
    width = gram_ref.shape[0]
    rows = lax.broadcasted_iota(jnp.int32, (width, width), 0)
    cols = lax.broadcasted_iota(jnp.int32, (width, width), 1)
    left[:, :width] = gram_ref[...]
    left[:, width:] = jnp.where(rows == cols, 1.0, 0.0)
    right[:, :width] = top_ref[...]
    right[:, width:] = jnp.zeros((width, width), jnp.float32)
    span = width + width // 2
    wide_row = lax.broadcasted_iota(jnp.int32, (block, span), 0)
    wide_col = lax.broadcasted_iota(jnp.int32, (block, span), 1)
    all_rows = lax.broadcasted_iota(jnp.int32, (width, block), 0)

    def window(start):
        return 0 if start < width // 2 else width // 2

    side = None
    for start in range(0, width + block, block):
        stop = start + block
        low = window(start)
        high_end = low + span
        old = start - block
        sweeps = []
        if start < width:
            sweeps.append(Sweep(left[start:stop, low:high_end], start - low, True, sub))
        if start:
            sweeps.append(Sweep(side, old - window(old), False, sub))
        for j in range(block):
            for sweep in sweeps:
                sweep.step(j)
        if start:
            side = sweeps[-1].panel * tiled(1.0 / sweeps[-1].pivots, span)
            others = jnp.where((all_rows < old) | (all_rows >= start), right[:, old:start], 0.0)
            place = slice(window(old), window(old) + span)
            right[:, place] = right[:, place] - product(others, side)
            right[old:start, place] = side
        if start < width:
            pivots = sweeps[0].pivots
            scale = lax.rsqrt(pivots)
            scale = scale * (1.5 - 0.5 * pivots * scale * scale)
            part = sweeps[0].panel * tiled(scale, span)
            part = jnp.where(wide_col + low >= wide_row + start, part, 0.0)
            if low:
                upper_ref[start:stop, :low] = jnp.zeros((block, low), jnp.float32)
            upper_ref[start:stop, low:] = part[:, : width - low]
            if stop < width:
                trail = product_tn(part[:, stop - low : width - low], part)
                left[stop:, low:high_end] = left[stop:, low:high_end] - trail
            side = right[start:stop, low:high_end] + part
    middle_ref[...] = right[:, width:]


def factor(gram, top):
    width = gram.shape[0]
    square = jax.ShapeDtypeStruct((width, width), jnp.float32)
    return pl.pallas_call(
        functools.partial(factor_kernel, block=64, sub=8),
        out_shape=(square, square),
        scratch_shapes=[pltpu.VMEM((width, 2 * width), jnp.float32)] * 2,
    )(gram, top)


def body(panel, trailing):
    row_count, width = panel.shape
    cols = lax.axis_size("col")
    row_index = lax.axis_index("row")
    col_index = lax.axis_index("col")
    core = row_index % 2
    piece_rows = row_count // cols
    part_rows = width // cols
    half_rows = part_rows // 2

    def cut(value, start, size):
        return lax.dynamic_slice_in_dim(value, start, size, 0)

    panel_piece = cut(panel, col_index * piece_rows, piece_rows)
    gram_here = product_tn(panel, panel)
    mine = col_index * part_rows + core * half_rows
    theirs = col_index * part_rows + (1 - core) * half_rows
    received = swapped(
        jnp.concatenate([cut(gram_here, theirs, half_rows), cut(panel, theirs, half_rows)], axis=0)
    )
    gram_half = cut(gram_here, mine, half_rows) + received[:half_rows]
    top_half = jnp.where(core == 0, cut(panel, mine, half_rows), received[half_rows:])
    stacked = gather_chips(jnp.concatenate([panel_piece, gram_half, top_half], axis=0))
    gram_half = jnp.sum(stacked[:, piece_rows : piece_rows + half_rows], axis=0)
    halves = jnp.concatenate([gram_half, stacked[0, piece_rows + half_rows :]], axis=0)
    received = spread(halves, stacked[:, :piece_rows])
    pair = jnp.stack(both_cores(received[:, piece_rows:]), axis=1)
    gram = pair[:, :, :half_rows].reshape(width, width)
    top_panel = pair[:, :, half_rows:].reshape(width, width)
    panel_cols = received[:, :piece_rows].reshape(row_count, width)
    panel_cols = jnp.concatenate(both_cores(panel_cols), axis=0)
    upper, middle = factor(gram, top_panel)
    band_block = -upper

    top_add = jnp.pad(upper, ((0, row_count - width), (0, 0)))
    vectors = panel + jnp.where(row_index == 0, top_add, 0.0)
    top_add = jnp.pad(upper, ((0, panel_cols.shape[0] - width), (0, 0)))
    vector_cols = panel_cols + jnp.where(col_index == 0, top_add, 0.0)

    partial = product(trailing, vector_cols, high)
    inner = product_tn(vectors, partial)
    sent = jnp.concatenate(
        [partial.reshape(cols, piece_rows, width), inner.reshape(cols, part_rows, width)], axis=1
    )
    summed = jnp.sum(lax.all_to_all(sent, "col", 0, 0), axis=0)
    image_piece = summed[:piece_rows]
    inner_part = summed[piece_rows:]
    stacked = gather_chips(jnp.concatenate([image_piece, inner_part], axis=0))
    inner_part = jnp.sum(stacked[:, piece_rows:], axis=0)
    received = spread(
        jnp.concatenate([inner_part, image_piece], axis=0), stacked[:, :piece_rows]
    )
    split = piece_rows + part_rows
    image = received[:, split:].reshape(row_count, width)
    first, second = both_cores(received[:, :split])
    inner = (first[:, piece_rows:] + second[:, piece_rows:]).reshape(width, width)
    image_cols = jnp.stack([first[:, :piece_rows], second[:, :piece_rows]])
    image_cols = image_cols.reshape(2 * row_count, width)

    half = 0.5 * product_tn(middle, product(inner, middle))
    correction = product(image, middle) - product(vectors, half)
    updated = trailing - product_nt(correction, vector_cols, high)
    correction_cols = product(image_cols, middle) - product(vector_cols, half)
    updated = updated - product_nt(vectors, correction_cols, high)
    return (band_block, updated)


def solution(mesh):
    in_specs = (P("row", None), P("row", "col"))
    out_specs = (P(), P("row", "col"))
    return jax.shard_map(body, mesh=mesh, in_specs=in_specs, out_specs=out_specs, check_vma=False)
```

```python
import functools

import jax
import jax.numpy as jnp
from jax import lax
from jax.experimental import pallas as pl
from jax.experimental.pallas import tpu as pltpu
from jax.sharding import PartitionSpec as P

highest = lax.Precision.HIGHEST
high = lax.Precision.HIGH


def product(left, right, precision=highest):
    return jnp.dot(left, right, precision=precision, preferred_element_type=jnp.float32)


def product_nt(left, right, precision=highest):
    return lax.dot_general(
        left,
        right,
        (((1,), (1,)), ((), ())),
        precision=precision,
        preferred_element_type=jnp.float32,
    )


def product_tn(left, right):
    return lax.dot_general(
        left, right, (((0,), (0,)), ((), ())), precision=highest, preferred_element_type=jnp.float32
    )


def swapped(value):
    return lax.ppermute(value, "row", [(i, i ^ 1) for i in range(lax.axis_size("row"))])


def both_cores(value):
    other = swapped(value)
    first = lax.axis_index("row") % 2 == 0
    return jnp.where(first, value, other), jnp.where(first, other, value)


def spread(value, own):
    copies = jnp.broadcast_to(value[None], (own.shape[0], *value.shape))
    return lax.all_to_all(jnp.concatenate([own, copies], axis=1), "col", 0, 0)


def gather_chips(value):
    chips = lax.axis_size("row") // 2
    groups = [[2 * z + k for z in range(chips)] for k in range(2)]
    return lax.all_gather(value, "row", axis=0, tiled=False, axis_index_groups=groups)


lanes = 128


def tiled(value, width):
    return jnp.concatenate([value] * (width // lanes), axis=1)


class Sweep:
    def __init__(self, panel, start, below, sub):
        self.panel, self.start, self.below, self.sub = panel, start, below, sub
        self.rows = panel.shape[0]
        self.place = lax.broadcasted_iota(jnp.int32, (self.rows, lanes), 0)
        self.pivots = jnp.zeros((self.rows, lanes), jnp.float32)

    def step(self, j):
        k = j % self.sub
        if k == 0:
            self.columns = [
                jnp.broadcast_to(self.panel[:, self.start + j + i : self.start + j + i + 1], (self.rows, lanes))
                for i in range(self.sub)
            ]
        column = self.columns[k]
        pivot = column[j : j + 1]
        keep = self.place > j if self.below else self.place != j
        ratio = jnp.where(keep, column * (1.0 / pivot), 0.0)
        for i in range(k + 1, self.sub):
            self.columns[i] = self.columns[i] - ratio * self.columns[i][j : j + 1]
        self.panel = self.panel - tiled(ratio, self.panel.shape[1]) * self.panel[j : j + 1]
        self.pivots = jnp.where(self.place == j, pivot, self.pivots)


def factor_kernel(gram_ref, top_ref, upper_ref, middle_ref, left, right, *, block, sub):
    width = gram_ref.shape[0]
    rows = lax.broadcasted_iota(jnp.int32, (width, width), 0)
    cols = lax.broadcasted_iota(jnp.int32, (width, width), 1)
    left[:, :width] = gram_ref[...]
    left[:, width:] = jnp.where(rows == cols, 1.0, 0.0)
    right[:, :width] = top_ref[...]
    right[:, width:] = jnp.zeros((width, width), jnp.float32)
    span = width + width // 2
    wide_row = lax.broadcasted_iota(jnp.int32, (block, span), 0)
    wide_col = lax.broadcasted_iota(jnp.int32, (block, span), 1)
    all_rows = lax.broadcasted_iota(jnp.int32, (width, block), 0)

    def window(start):
        return 0 if start < width // 2 else width // 2

    side = None
    for start in range(0, width + block, block):
        stop = start + block
        low = window(start)
        high_end = low + span
        old = start - block
        sweeps = []
        if start < width:
            sweeps.append(Sweep(left[start:stop, low:high_end], start - low, True, sub))
        if start:
            sweeps.append(Sweep(side, old - window(old), False, sub))
        for j in range(block):
            for sweep in sweeps:
                sweep.step(j)
        if start:
            side = sweeps[-1].panel * tiled(1.0 / sweeps[-1].pivots, span)
            others = jnp.where((all_rows < old) | (all_rows >= start), right[:, old:start], 0.0)
            place = slice(window(old), window(old) + span)
            right[:, place] = right[:, place] - product(others, side)
            right[old:start, place] = side
        if start < width:
            pivots = sweeps[0].pivots
            scale = lax.rsqrt(pivots)
            scale = scale * (1.5 - 0.5 * pivots * scale * scale)
            part = sweeps[0].panel * tiled(scale, span)
            part = jnp.where(wide_col + low >= wide_row + start, part, 0.0)
            if low:
                upper_ref[start:stop, :low] = jnp.zeros((block, low), jnp.float32)
            upper_ref[start:stop, low:] = part[:, : width - low]
            if stop < width:
                trail = product_tn(part[:, stop - low : width - low], part)
                left[stop:, low:high_end] = left[stop:, low:high_end] - trail
            side = right[start:stop, low:high_end] + part
    middle_ref[...] = right[:, width:]


def factor(gram, top):
    width = gram.shape[0]
    square = jax.ShapeDtypeStruct((width, width), jnp.float32)
    return pl.pallas_call(
        functools.partial(factor_kernel, block=64, sub=8),
        out_shape=(square, square),
        scratch_shapes=[pltpu.VMEM((width, 2 * width), jnp.float32)] * 2,
    )(gram, top)


def body(panel, trailing):
    row_count, width = panel.shape
    cols = lax.axis_size("col")
    row_index = lax.axis_index("row")
    col_index = lax.axis_index("col")
    core = row_index % 2
    piece_rows = row_count // cols
    part_rows = width // cols
    half_rows = part_rows // 2

    def cut(value, start, size):
        return lax.dynamic_slice_in_dim(value, start, size, 0)

    panel_piece = cut(panel, col_index * piece_rows, piece_rows)
    gram_here = product_tn(panel, panel)
    mine = col_index * part_rows + core * half_rows
    theirs = col_index * part_rows + (1 - core) * half_rows
    received = swapped(
        jnp.concatenate([cut(gram_here, theirs, half_rows), cut(panel, theirs, half_rows)], axis=0)
    )
    gram_half = cut(gram_here, mine, half_rows) + received[:half_rows]
    top_half = jnp.where(core == 0, cut(panel, mine, half_rows), received[half_rows:])
    stacked = gather_chips(jnp.concatenate([panel_piece, gram_half, top_half], axis=0))
    gram_half = jnp.sum(stacked[:, piece_rows : piece_rows + half_rows], axis=0)
    halves = jnp.concatenate([gram_half, stacked[0, piece_rows + half_rows :]], axis=0)
    received = spread(halves, stacked[:, :piece_rows])
    first, second = both_cores(received)
    pair = jnp.stack([first, second], axis=1)
    gram = pair[:, :, piece_rows : piece_rows + half_rows].reshape(width, width)
    top_panel = pair[:, :, piece_rows + half_rows :].reshape(width, width)
    panel_cols = jnp.stack([first[:, :piece_rows], second[:, :piece_rows]])
    panel_cols = panel_cols.reshape(2 * row_count, width)
    upper, middle = factor(gram, top_panel)
    band_block = -upper

    top_add = jnp.pad(upper, ((0, row_count - width), (0, 0)))
    vectors = panel + jnp.where(row_index == 0, top_add, 0.0)
    top_add = jnp.pad(upper, ((0, panel_cols.shape[0] - width), (0, 0)))
    vector_cols = panel_cols + jnp.where(col_index == 0, top_add, 0.0)

    partial = product(trailing, vector_cols, high)
    inner = product_tn(vectors, partial)
    sent = jnp.concatenate(
        [partial.reshape(cols, piece_rows, width), inner.reshape(cols, part_rows, width)], axis=1
    )
    summed = jnp.sum(lax.all_to_all(sent, "col", 0, 0), axis=0)
    image_piece = summed[:piece_rows]
    inner_part = summed[piece_rows:]
    stacked = gather_chips(jnp.concatenate([image_piece, inner_part], axis=0))
    inner_part = jnp.sum(stacked[:, piece_rows:], axis=0)
    received = spread(
        jnp.concatenate([inner_part, image_piece], axis=0), stacked[:, :piece_rows]
    )
    split = piece_rows + part_rows
    image = received[:, split:].reshape(row_count, width)
    first, second = both_cores(received[:, :split])
    inner = (first[:, piece_rows:] + second[:, piece_rows:]).reshape(width, width)
    image_cols = jnp.stack([first[:, :piece_rows], second[:, :piece_rows]])
    image_cols = image_cols.reshape(2 * row_count, width)

    updated = trailing - product_nt(product(image, middle), vector_cols, high)
    core_square = product_tn(middle, product(inner, middle))
    correction_cols = product(image_cols, middle) - product(vector_cols, core_square)
    updated = updated - product_nt(vectors, correction_cols, high)
    return (band_block, updated)


def solution(mesh):
    in_specs = (P("row", None), P("row", "col"))
    out_specs = (P(), P("row", "col"))
    return jax.shard_map(body, mesh=mesh, in_specs=in_specs, out_specs=out_specs, check_vma=False)
```

```python
import functools

import jax
import jax.numpy as jnp
from jax import lax
from jax.experimental import pallas as pl
from jax.experimental.pallas import tpu as pltpu
from jax.sharding import PartitionSpec as P

highest = lax.Precision.HIGHEST
high = lax.Precision.HIGH


def product(left, right, precision=highest):
    return jnp.dot(left, right, precision=precision, preferred_element_type=jnp.float32)


def product_nt(left, right, precision=highest):
    return lax.dot_general(
        left,
        right,
        (((1,), (1,)), ((), ())),
        precision=precision,
        preferred_element_type=jnp.float32,
    )


def product_tn(left, right):
    return lax.dot_general(
        left, right, (((0,), (0,)), ((), ())), precision=highest, preferred_element_type=jnp.float32
    )


def swapped(value):
    return lax.ppermute(value, "row", [(i, i ^ 1) for i in range(lax.axis_size("row"))])


def both_cores(value):
    other = swapped(value)
    first = lax.axis_index("row") % 2 == 0
    return jnp.where(first, value, other), jnp.where(first, other, value)


def spread(value, own):
    copies = jnp.broadcast_to(value[None], (own.shape[0], *value.shape))
    return lax.all_to_all(jnp.concatenate([own, copies], axis=1), "col", 0, 0)


def gather_chips(value):
    chips = lax.axis_size("row") // 2
    groups = [[2 * z + k for z in range(chips)] for k in range(2)]
    return lax.all_gather(value, "row", axis=0, tiled=False, axis_index_groups=groups)


lanes = 128


def tiled(value, width):
    return jnp.concatenate([value] * (width // lanes), axis=1)


class Sweep:
    def __init__(self, panel, start, below, sub):
        self.panel, self.start, self.below, self.sub = panel, start, below, sub
        self.rows = panel.shape[0]
        self.place = lax.broadcasted_iota(jnp.int32, (self.rows, lanes), 0)
        self.pivots = jnp.zeros((self.rows, lanes), jnp.float32)

    def step(self, j):
        k = j % self.sub
        if k == 0:
            self.columns = [
                jnp.broadcast_to(self.panel[:, self.start + j + i : self.start + j + i + 1], (self.rows, lanes))
                for i in range(self.sub)
            ]
        column = self.columns[k]
        pivot = column[j : j + 1]
        keep = self.place > j if self.below else self.place != j
        ratio = jnp.where(keep, column * (1.0 / pivot), 0.0)
        for i in range(k + 1, self.sub):
            self.columns[i] = self.columns[i] - ratio * self.columns[i][j : j + 1]
        self.panel = self.panel - tiled(ratio, self.panel.shape[1]) * self.panel[j : j + 1]
        self.pivots = jnp.where(self.place == j, pivot, self.pivots)


def factor_kernel(gram_ref, top_ref, upper_ref, middle_ref, left, right, *, block, sub):
    width = gram_ref.shape[0]
    rows = lax.broadcasted_iota(jnp.int32, (width, width), 0)
    cols = lax.broadcasted_iota(jnp.int32, (width, width), 1)
    left[:, :width] = gram_ref[...]
    left[:, width:] = jnp.where(rows == cols, 1.0, 0.0)
    right[:, :width] = top_ref[...]
    right[:, width:] = jnp.zeros((width, width), jnp.float32)
    span = width + width // 2
    wide_row = lax.broadcasted_iota(jnp.int32, (block, span), 0)
    wide_col = lax.broadcasted_iota(jnp.int32, (block, span), 1)
    all_rows = lax.broadcasted_iota(jnp.int32, (width, block), 0)

    def window(start):
        return 0 if start < width // 2 else width // 2

    side = None
    for start in range(0, width + block, block):
        stop = start + block
        low = window(start)
        high_end = low + span
        old = start - block
        sweeps = []
        if start < width:
            sweeps.append(Sweep(left[start:stop, low:high_end], start - low, True, sub))
        if start:
            sweeps.append(Sweep(side, old - window(old), False, sub))
        for j in range(block):
            for sweep in sweeps:
                sweep.step(j)
        if start:
            side = sweeps[-1].panel * tiled(1.0 / sweeps[-1].pivots, span)
            others = jnp.where((all_rows < old) | (all_rows >= start), right[:, old:start], 0.0)
            place = slice(window(old), window(old) + span)
            right[:, place] = right[:, place] - product(others, side)
            right[old:start, place] = side
        if start < width:
            pivots = sweeps[0].pivots
            scale = lax.rsqrt(pivots)
            scale = scale * (1.5 - 0.5 * pivots * scale * scale)
            part = sweeps[0].panel * tiled(scale, span)
            part = jnp.where(wide_col + low >= wide_row + start, part, 0.0)
            if low:
                upper_ref[start:stop, :low] = jnp.zeros((block, low), jnp.float32)
            upper_ref[start:stop, low:] = part[:, : width - low]
            if stop < width:
                trail = product_tn(part[:, stop - low : width - low], part)
                left[stop:, low:high_end] = left[stop:, low:high_end] - trail
            side = right[start:stop, low:high_end] + part
    middle_ref[...] = right[:, width:]


def factor(gram, top):
    width = gram.shape[0]
    square = jax.ShapeDtypeStruct((width, width), jnp.float32)
    return pl.pallas_call(
        functools.partial(factor_kernel, block=64, sub=8),
        out_shape=(square, square),
        scratch_shapes=[pltpu.VMEM((width, 2 * width), jnp.float32)] * 2,
    )(gram, top)


def body(panel, trailing):
    row_count, width = panel.shape
    cols = lax.axis_size("col")
    row_index = lax.axis_index("row")
    col_index = lax.axis_index("col")
    core = row_index % 2
    piece_rows = row_count // cols
    part_rows = width // cols
    half_rows = part_rows // 2

    def cut(value, start, size):
        return lax.dynamic_slice_in_dim(value, start, size, 0)

    panel_piece = cut(panel, col_index * piece_rows, piece_rows)
    gram_here = product_tn(panel, panel)
    mine = col_index * part_rows + core * half_rows
    theirs = col_index * part_rows + (1 - core) * half_rows
    received = swapped(
        jnp.concatenate([cut(gram_here, theirs, half_rows), cut(panel, theirs, half_rows)], axis=0)
    )
    gram_half = cut(gram_here, mine, half_rows) + received[:half_rows]
    top_half = jnp.where(core == 0, cut(panel, mine, half_rows), received[half_rows:])
    stacked = gather_chips(jnp.concatenate([panel_piece, gram_half, top_half], axis=0))
    gram_half = jnp.sum(stacked[:, piece_rows : piece_rows + half_rows], axis=0)
    halves = jnp.concatenate([gram_half, stacked[0, piece_rows + half_rows :]], axis=0)
    received = spread(halves, stacked[:, :piece_rows])
    first, second = both_cores(received)
    pair = jnp.stack([first, second], axis=1)
    gram = pair[:, :, piece_rows : piece_rows + half_rows].reshape(width, width)
    top_panel = pair[:, :, piece_rows + half_rows :].reshape(width, width)
    panel_cols = jnp.stack([first[:, :piece_rows], second[:, :piece_rows]])
    panel_cols = panel_cols.reshape(2 * row_count, width)
    upper, middle = factor(gram, top_panel)
    band_block = -upper

    top_add = jnp.pad(upper, ((0, row_count - width), (0, 0)))
    vectors = panel + jnp.where(row_index == 0, top_add, 0.0)
    top_add = jnp.pad(upper, ((0, panel_cols.shape[0] - width), (0, 0)))
    vector_cols = panel_cols + jnp.where(col_index == 0, top_add, 0.0)

    partial = product(trailing, vector_cols, high)
    inner = product_tn(vectors, partial)
    sent = jnp.concatenate(
        [partial.reshape(cols, piece_rows, width), inner.reshape(cols, part_rows, width)], axis=1
    )
    summed = jnp.sum(lax.all_to_all(sent, "col", 0, 0), axis=0)
    image_piece = summed[:piece_rows]
    inner_part = summed[piece_rows:]
    stacked = gather_chips(jnp.concatenate([image_piece, inner_part], axis=0))
    inner_part = jnp.sum(stacked[:, piece_rows:], axis=0)
    received = spread(
        jnp.concatenate([inner_part, image_piece], axis=0), stacked[:, :piece_rows]
    )
    split = piece_rows + part_rows
    image = received[:, split:].reshape(row_count, width)
    first, second = both_cores(received[:, :split])
    inner = (first[:, piece_rows:] + second[:, piece_rows:]).reshape(width, width)
    image_cols = jnp.stack([first[:, :piece_rows], second[:, :piece_rows]])
    image_cols = image_cols.reshape(2 * row_count, width)

    updated = trailing - product_nt(product(image, middle, high), vector_cols, high)
    core_square = product_tn(middle, product(inner, middle))
    correction_cols = product(image_cols, middle, high) - product(
        vector_cols, core_square, high
    )
    updated = updated - product_nt(vectors, correction_cols, high)
    return (band_block, updated)


def solution(mesh):
    in_specs = (P("row", None), P("row", "col"))
    out_specs = (P(), P("row", "col"))
    return jax.shard_map(body, mesh=mesh, in_specs=in_specs, out_specs=out_specs, check_vma=False)
```
